32 devices in a mesh: gx: 4 (over z), gy: 2 (over x), sa: 4 (over y, core).
Axes of the slice: x: 2, y: 2, z: 4, core: 2. Of those that a mesh axis runs over, the one named last changes fastest.
Arguments:
- profile_fields: float32 [32, 4, 32768], P(None, None, ('gx', 'gy', 'sa')), may hold values from -6 to 6
- turbulent_coefficients: float32 [32, 2, 32768], P(None, None, ('gx', 'gy', 'sa')), may hold values from 0.3 to 6
- column_patch_owner: int32 [2, 32768], P(None, ('gx', 'gy', 'sa')), may hold values from 0 to 1023, as said below
- kind_fractions: float32 [6, 32768], P(None, ('gx', 'gy', 'sa')), may hold values from 0.1 to 1
- kind_existing_flags: int32 [5, 32768], P(None, ('gx', 'gy', 'sa')), may hold values 0 or 1
- kind_absorbed_flux: float32 [6, 32768], P(None, ('gx', 'gy', 'sa')), may hold values from -6 to 6
- kind_thermal_links: float32 [6, 32768], P(None, ('gx', 'gy', 'sa')), may hold values from 0.2 to 3
- bottom_kelvin: float32 [6, 32768], P(None, ('gx', 'gy', 'sa')), may hold values from -5 to 5
- drift_speeds: float32 [2, 32768], P(None, ('gx', 'gy', 'sa')), may hold values from -5 to 5
Outputs:
- advanced_profile: float32 [32, 4, 32768], P(None, None, ('gx', 'gy', 'sa'))
- kind_interface_kelvin: float32 [6, 32768], P(None, ('gx', 'gy', 'sa'))
The draws below stay inside these ranges and needn't reach their ends.
Inputs may be any that keep to these rules, and one draw needn't show every extreme that they name: column_patch_owner[0, i] * 1024 + column_patch_owner[1, i] over all columns i is a permutation of the 32768 cells; row 0 is below 32 and row 1 below 1024. Cell j is held by the device that holds entry j of the cell arrays. The columns of one device have their cells on every device, 1 to 64 of them on each, and exactly 64 on some device.
All inputs are finite; a program needn't handle non-finite values. No bound on the sum of `kind_existing_flags` on one device may be relied on, other than what follows from the above.
Results may differ from the reference program's by a relative error of at most 0.00016.
Values sent between devices are 32-bit elements; how exact they have to be, the bound alone decides.
A program may use at most 64 MiB of HBM per device.

```python
import math
import jax
import jax.numpy as jnp
from jax import lax

COL_DEV = 1024
LEV = 32
SWEEPS = 3
COLS = 32768
GROUND_PATCHES = 32768
CAP = 64


def draw_column_patch_owner(key, part):
    device_total = COLS // COL_DEV
    unit_total = device_total * (CAP - 1)
    base_key = jax.random.fold_in(key, 17)
    subkeys = jax.random.split(base_key, 6)
    full_group = jax.random.randint(subkeys[0], (), 0, device_total)
    unit_ids = jnp.arange(unit_total, dtype=jnp.int32)
    scores = jax.random.randint(subkeys[1], (unit_total,), 0, unit_total) * unit_total + unit_ids
    scores = jnp.where(unit_ids // (CAP - 1) == full_group, unit_ids - unit_total * unit_total, scores)
    ranked = jnp.argsort(scores)
    chosen = jnp.zeros((unit_total,), jnp.int32).at[ranked[:COL_DEV - device_total]].set(1)
    group_sizes = 1 + jnp.sum(chosen.reshape(device_total, CAP - 1), axis=1)
    group_ends = jnp.cumsum(group_sizes)
    position = jnp.arange(COL_DEV, dtype=jnp.int32)
    group_of = jnp.sum((position[:, None] >= group_ends[None, :]).astype(jnp.int32), axis=1)
    source_rank = jax.random.permutation(subkeys[2], device_total)
    owner_perm = jax.random.permutation(subkeys[3], device_total)
    owner_dev = owner_perm[(source_rank[:, None] + group_of[None, :]) % device_total]
    slot_perm = jax.vmap(lambda subkey: jax.random.permutation(subkey, COL_DEV))(jax.random.split(subkeys[4], device_total))
    cell_local = slot_perm.reshape(-1)[owner_dev * COL_DEV + position[None, :]]
    column_perm = jax.vmap(lambda subkey: jax.random.permutation(subkey, COL_DEV))(jax.random.split(subkeys[5], device_total))
    owner_out = jnp.take_along_axis(owner_dev, column_perm, axis=1).reshape(-1)
    local_out = jnp.take_along_axis(cell_local, column_perm, axis=1).reshape(-1)
    return jnp.stack([owner_out, local_out], axis=0).astype(jnp.int32)


def place_ends(array, stream_key, least, top_value):
    index_at = [jax.random.randint(jax.random.fold_in(stream_key, axis), (), 0, length) for axis, length in enumerate(array.shape)]
    main_axis = array.shape.index(max(array.shape))
    neighbour = index_at[:main_axis] + [(index_at[main_axis] + 1) % array.shape[main_axis]] + index_at[main_axis + 1:]
    return array.at[tuple(index_at)].set(least).at[tuple(neighbour)].set(top_value)


def steps_of(rng, dims, cuts, low, high):
    loudness = 1.0
    for dim, blocks in cuts:
        draws = jax.random.uniform(jax.random.fold_in(jax.random.fold_in(rng, 6), dim), (blocks,), jnp.float32, low / len(cuts), high / len(cuts))
        loudness = loudness * jnp.repeat(jnp.exp(draws), dims[dim] // blocks).reshape((-1,) + (1,) * (len(dims) - 1 - dim))
    return loudness


def normal_values(own_key, shape, spread, bound, shards=(), kind=jnp.bfloat16):
    result = spread * jax.random.normal(own_key, shape, jnp.float32)
    if shards:
        result = result * steps_of(own_key, shape, shards, -0.22, 0.18)
    return jnp.clip(result, -bound, bound).astype(kind)


def setup_inputs(seed: int = 0) -> dict:
    key_of = jax.random.split(jax.random.key(seed), 10)
    profile_fields = normal_values(key_of[0], (LEV, 4, COLS), 1.0, 6.0, ((2, 32),), jnp.float32)
    turbulent_coefficients = jnp.clip(jnp.exp(math.log(6.0) - 2.9957322 * jax.random.uniform(key_of[1], (LEV, 2, COLS), jnp.float32) ** steps_of(key_of[1], (LEV, 2, COLS), ((2, 32),), -0.2, 0.2)), 0.3, 6.0)
    column_patch_owner = draw_column_patch_owner(jax.random.fold_in(key_of[9], 71), 0)
    kind_fractions = jnp.clip(jnp.exp(math.log(1.0) - 2.3025851 * jax.random.uniform(key_of[3], (6, GROUND_PATCHES), jnp.float32) ** steps_of(key_of[3], (6, GROUND_PATCHES), ((1, 32),), -0.2, 0.2)), 0.1, 1.0)
    kind_existing_flags = place_ends((jax.random.randint(key_of[4], (5, GROUND_PATCHES), 0, 2) < 1).astype(jnp.int32), jax.random.fold_in(key_of[4], 1), 0, 1)
    kind_absorbed_flux = normal_values(key_of[5], (6, GROUND_PATCHES), 1.5, 6.0, ((1, 32),), jnp.float32)
    kind_thermal_links = jnp.clip(jnp.exp(math.log(3.0) - 2.7080502 * jax.random.uniform(key_of[6], (6, GROUND_PATCHES), jnp.float32) ** steps_of(key_of[6], (6, GROUND_PATCHES), ((1, 32),), -0.2, 0.2)), 0.2, 3.0)
    bottom_kelvin = normal_values(key_of[7], (6, GROUND_PATCHES), 1.0, 5.0, ((1, 32),), jnp.float32)
    drift_speeds = normal_values(key_of[8], (2, GROUND_PATCHES), 1.0, 5.0, ((1, 32),), jnp.float32)
    return dict(profile_fields=profile_fields, turbulent_coefficients=turbulent_coefficients, column_patch_owner=column_patch_owner, kind_fractions=kind_fractions, kind_existing_flags=kind_existing_flags, kind_absorbed_flux=kind_absorbed_flux, kind_thermal_links=kind_thermal_links, bottom_kelvin=bottom_kelvin, drift_speeds=drift_speeds)


VAPOUR_ENTHALPY = 2.5


def vapour_limit(values):
    return 0.6 * jnp.exp(0.3 * values)


def longwave_outgoing(values):
    return 0.5 * jnp.exp(0.2 * values)


def eliminate(values, coupling):
    def advance(carried, inputs):
        offset_prev, factor_prev, above_coef = carried
        level_values, below_coef = inputs
        divisor = 1.0 + above_coef * (1.0 - factor_prev) + below_coef
        offset_now = (level_values + above_coef * offset_prev) / divisor
        factor_now = below_coef / divisor
        return (offset_now, factor_now, below_coef), (offset_now, factor_now)

    zeros_row = jnp.zeros_like(values[0])
    _, (sweep_shifts, sweep_multipliers) = lax.scan(advance, (zeros_row, zeros_row, zeros_row), (values, coupling))
    return sweep_shifts, sweep_multipliers


def substitute(sweep_shifts, sweep_multipliers, boundary):
    def advance(level_below, inputs):
        level_offset, level_factor = inputs
        solved = level_offset + level_factor * level_below
        return solved, solved

    _, solved = lax.scan(advance, boundary, (sweep_shifts, sweep_multipliers), reverse=True)
    return solved


def surface_weights(kind_fractions, kind_existing_flags):
    present = jnp.concatenate([jnp.ones_like(kind_existing_flags[:1]), kind_existing_flags], axis=0).astype(kind_fractions.dtype)
    unscaled = kind_fractions * present
    return unscaled / jnp.sum(unscaled, axis=0, keepdims=True)


def flux_budget(cell_fields, heat_offset, heat_factor, moist_offset, moist_factor, transfer_factor):
    fraction_shares = cell_fields[0:6]
    absorbed_flux = cell_fields[6:12]
    thermal_link = cell_fields[12:18]
    bottom_layer = cell_fields[18:24]
    interface_kelvin = bottom_layer
    for sweep_index in range(SWEEPS):
        humidity_limit = vapour_limit(interface_kelvin)
        averaged_enthalpy = jnp.sum(fraction_shares * interface_kelvin, axis=0)
        averaged_humidity = jnp.sum(fraction_shares * humidity_limit, axis=0)
        lowest_enthalpy = heat_offset + heat_factor * averaged_enthalpy
        lowest_humidity = moist_offset + moist_factor * averaged_humidity
        outgoing_flux = longwave_outgoing(interface_kelvin)
        budget_residual = (absorbed_flux - outgoing_flux - transfer_factor * (interface_kelvin - lowest_enthalpy)
                     - VAPOUR_ENTHALPY * transfer_factor * (humidity_limit - lowest_humidity) - thermal_link * (interface_kelvin - bottom_layer))
        budget_slope = 0.2 * outgoing_flux + transfer_factor * (1.0 + VAPOUR_ENTHALPY * 0.3 * humidity_limit) + thermal_link
        interface_kelvin = interface_kelvin + budget_residual / budget_slope
    humidity_limit = vapour_limit(interface_kelvin)
    return interface_kelvin, jnp.sum(fraction_shares * interface_kelvin, axis=0), jnp.sum(fraction_shares * humidity_limit, axis=0)


def reference(profile_fields, turbulent_coefficients, column_patch_owner, kind_fractions, kind_existing_flags, kind_absorbed_flux, kind_thermal_links, bottom_kelvin, drift_speeds):
    coupling = jnp.repeat(turbulent_coefficients, 2, axis=1)
    sweep_shifts, sweep_multipliers = eliminate(profile_fields, coupling)
    fraction_shares = surface_weights(kind_fractions, kind_existing_flags)
    patch_locator = (column_patch_owner[0] * COL_DEV + column_patch_owner[1]).astype(jnp.int32)
    patch_directory = jnp.concatenate([fraction_shares, kind_absorbed_flux, kind_thermal_links, bottom_kelvin, drift_speeds], axis=0)
    gathered_fields = patch_directory[:, patch_locator]
    interface_kelvin, averaged_enthalpy, averaged_humidity = flux_budget(gathered_fields, sweep_shifts[-1, 0], sweep_multipliers[-1, 0], sweep_shifts[-1, 1], sweep_multipliers[-1, 1], turbulent_coefficients[-1, 0])
    kind_interface_kelvin = jnp.zeros_like(bottom_kelvin).at[:, patch_locator].set(interface_kelvin)
    boundary = jnp.stack([averaged_enthalpy, averaged_humidity, gathered_fields[24], gathered_fields[25]], axis=0)
    advanced_profile = substitute(sweep_shifts, sweep_multipliers, boundary)
    return advanced_profile, kind_interface_kelvin
```

```python
import functools

import jax
import jax.numpy as jnp
from jax import lax
from jax.experimental import pallas as pl
from jax.experimental.pallas import tpu as pltpu
from jax.sharding import PartitionSpec as P

SWEEPS = 3
AXES = ("gx", "gy", "sa")
LANES = 128
HALF = LANES // 2
GROUP = 32
F32, BF16, I32 = jnp.float32, jnp.bfloat16, jnp.int32
NT = (((1,), (1,)), ((), ()))
NN = (((1,), (0,)), ((), ()))


def dot(a, b, dims):
    return lax.dot_general(a, b, dims, preferred_element_type=F32)


def halves(x):
    high = x.astype(BF16).astype(F32)
    return high, x - high


def one_hot(mask):
    return jnp.where(mask, 1.0, 0.0).astype(BF16)


def kernel(
    sizes,
    prof_hbm, turb_hbm, owner_hbm, frac_hbm, flag_hbm, flux_hbm, link_hbm, base_hbm, drift_hbm,
    adv_hbm, kelvin_hbm,
    prof, turb, owner_v, frac, flag, flux, link, base, drift,
    fac, kelvin, rout, lhs, near, code_h, send1, recv1, send2, recv2,
    in_sem, lev_sem, out_sem, s1, r1, s2, r2,
):
    gx, gy, sa, levels, cols, pieces = sizes
    n = gx * gy * sa
    blocks = cols // LANES
    groups = n // GROUP
    step = levels // pieces
    me = (lax.axis_index("gx") * gy + lax.axis_index("gy")) * sa + lax.axis_index("sa")

    def coords(o):
        q = (me + o) % n
        return q, (q // (gy * sa), (q // sa) % gy, q % sa)

    def peers(fn):
        if n <= GROUP:
            for o in range(1, n):
                fn(o)
        else:
            def body(o, c):
                fn(o)
                return c
            lax.fori_loop(1, n, body, 0)

    def each_group(fn, init):
        if groups == 1:
            return fn(0, init)
        return lax.fori_loop(0, groups, fn, init)

    barrier = pltpu.get_barrier_semaphore()
    peers(lambda o: pl.semaphore_signal(
        barrier, inc=1, device_id=coords(o)[1], device_id_type=pl.DeviceIdType.MESH))

    loads = [
        pltpu.make_async_copy(a, b, in_sem.at[i])
        for i, (a, b) in enumerate((
            (owner_hbm, owner_v), (frac_hbm, frac), (flag_hbm, flag), (flux_hbm, flux),
            (link_hbm, link), (base_hbm, base), (drift_hbm, drift)))
    ]
    loads[0].start()
    lev_loads = []
    for i in range(pieces):
        rows = pl.ds(i * step, step)
        lev_loads.append((
            pltpu.make_async_copy(turb_hbm.at[rows], turb.at[rows], lev_sem.at[0, i]),
            pltpu.make_async_copy(prof_hbm.at[rows], prof.at[rows], lev_sem.at[1, i])))
        for c in lev_loads[-1]:
            c.start()
    for c in loads[1:]:
        c.start()

    loads[0].wait()
    owner = owner_v[0:1, :]
    local = owner_v[1:2, :]
    onehot_d = lax.broadcasted_iota(I32, (n, cols), 0) == owner
    d01 = one_hot(onehot_d)
    stacked = jnp.concatenate([d01[:, b * LANES:(b + 1) * LANES] for b in range(blocks)], axis=0)
    ti = lax.broadcasted_iota(I32, (LANES, 2 * LANES), 0)
    tj = lax.broadcasted_iota(I32, (LANES, 2 * LANES), 1)
    tri = one_hot((ti < tj) | (tj >= LANES))
    counts = dot(stacked, tri, NN)
    carry = jnp.zeros((n, LANES), F32)
    ranks = []
    for b in range(blocks):
        part = counts[b * n:(b + 1) * n]
        mask = onehot_d[:, b * LANES:(b + 1) * LANES]
        ranks.append(jnp.sum(jnp.where(mask, part[:, :LANES] + carry, 0.0), axis=0, keepdims=True))
        carry = carry + part[:, LANES:]
    rank = jnp.concatenate(ranks, axis=1).astype(I32)
    r01 = one_hot(lax.broadcasted_iota(I32, (HALF, cols), 0) == rank)
    zero = jnp.zeros((HALF, cols), BF16)
    for i in range(2):
        rout[pl.ds(i * LANES, HALF), 0:cols] = r01
        rout[pl.ds(i * LANES, HALF), cols:2 * cols] = zero
        rout[pl.ds(i * LANES + HALF, HALF), 0:cols] = zero
        rout[pl.ds(i * LANES + HALF, HALF), cols:2 * cols] = r01

    def eliminate(row, v, wait):
        above = off = factor = None
        for k in range(levels):
            if wait and k % step == 0:
                for c in lev_loads[k // step]:
                    c.wait()
            below = jnp.broadcast_to(turb[k, row:row + 1, :], (2, cols))
            x = prof[k, v:v + 2, :]
            if k == 0:
                inv = 1.0 / (1.0 + below)
                off = x * inv
            else:
                inv = 1.0 / (1.0 + above * (1.0 - factor) + below)
                off = (x + above * off) * inv
            factor = below * inv
            above = below
            prof[k, v:v + 2, :] = off
            fac[k, v:v + 2, :] = factor
        return off, factor, below

    off, factor, below = eliminate(0, 0, True)
    code = (local + 1).astype(F32)
    blank = jnp.zeros_like(code)
    even = jnp.concatenate([off[0:1], factor[0:1], code, blank], axis=0)
    odd = jnp.concatenate([off[1:2], below[1:2], code, blank], axis=0)
    wide = jnp.concatenate([
        jnp.concatenate(halves(even), axis=0), jnp.concatenate(halves(odd), axis=0)], axis=1)
    owner8 = jnp.broadcast_to(owner, (8, cols))

    def dispatch(g, c):
        for t in range(GROUP // 2):
            parts = []
            for u in range(2):
                m = owner8 == g * GROUP + 2 * t + u
                parts.append(jnp.where(jnp.concatenate([m, m], axis=1), wide, 0.0))
            lhs[pl.ds(16 * t, 16), :] = jnp.concatenate(parts, axis=0).astype(BF16)
        out = dot(lhs[...], rout[0:LANES, :], NT)
        for d in range(GROUP):
            send1[g * GROUP + d] = out[8 * d:8 * d + 4] + out[8 * d + 4:8 * d + 8]
        return c

    each_group(dispatch, 0)
    recv1[me] = send1[me]

    pl.semaphore_wait(barrier, n - 1)

    def send(src, dst, ss, rs):
        def one(o):
            q, where = coords(o)
            pltpu.make_async_remote_copy(
                src_ref=src.at[q], dst_ref=dst.at[me], send_sem=ss, recv_sem=rs,
                device_id=where, device_id_type=pl.DeviceIdType.MESH).start()
        peers(one)

    def wait_all(buf, sem):
        part = buf.at[pl.ds(0, n - 1)]
        pltpu.make_async_copy(part, part, sem).wait()

    send(send1, recv1, s1, r1)

    eliminate(1, 2, False)
    for c in loads[1:]:
        c.wait()
    present = jnp.concatenate(
        [jnp.ones((1, cols), F32), flag[...].astype(F32)], axis=0)
    share = frac[...] * present
    share = share / jnp.sum(share, axis=0, keepdims=True)

    wait_all(recv1, r1)
    lane = lax.broadcasted_iota(I32, (4, LANES), 1)
    left = lane < HALF
    slots = GROUP * HALF

    def collect(g, acc):
        evens, odds = [], []
        for m in range(GROUP // 2):
            a = recv1[g * GROUP + 2 * m]
            b = recv1[g * GROUP + 2 * m + 1]
            evens.append(jnp.where(left, a, pltpu.roll(b, HALF, 1)))
            odds.append(jnp.where(left, pltpu.roll(a, HALF, 1), b))
        even = jnp.concatenate(evens, axis=1)
        odd = jnp.concatenate(odds, axis=1)
        at = even[2:3].astype(I32) - 1
        high, low = halves(jnp.concatenate([even[0:2], odd[0:2]], axis=0))
        v = jnp.concatenate([high, low], axis=0)
        at8 = jnp.broadcast_to(at, (8, slots))
        far = at8 // LANES
        far = jnp.where(at8 < 0, -1, far)
        code_h[g] = far
        within = at - far[0:1] * LANES
        jl = one_hot(lax.broadcasted_iota(I32, (LANES, slots), 0) == within)
        near[g] = jl
        rows = jnp.concatenate(
            [jnp.where(far == h, v, 0.0) for h in range(blocks)], axis=0).astype(BF16)
        return acc + dot(rows, jl, NT)

    got = each_group(collect, jnp.zeros((8 * blocks, LANES), F32))
    x = jnp.concatenate(
        [got[8 * h:8 * h + 4] + got[8 * h + 4:8 * h + 8] for h in range(blocks)], axis=1)
    kinds = base.shape[0]
    off_h, fac_s, off_m, exch = [jnp.broadcast_to(x[i:i + 1], (kinds, cols)) for i in range(4)]
    bottom = base[...]
    absorbed = flux[...]
    coupled = link[...]
    temp = bottom
    for _ in range(SWEEPS):
        sat = 0.6 * jnp.exp(0.3 * temp)
        mean_heat = jnp.sum(share * temp, axis=0, keepdims=True)
        mean_moist = jnp.sum(share * sat, axis=0, keepdims=True)
        air_heat = off_h + fac_s * mean_heat
        air_moist = off_m + fac_s * mean_moist
        emitted = 0.5 * jnp.exp(0.2 * temp)
        imbalance = (absorbed - emitted - exch * (temp - air_heat)
                     - 2.5 * exch * (sat - air_moist) - coupled * (temp - bottom))
        slope = 0.2 * emitted + exch * (1.0 + 2.5 * 0.3 * sat) + coupled
        temp = temp + imbalance / slope
    kelvin[...] = temp
    sat = 0.6 * jnp.exp(0.3 * temp)
    mean_heat = jnp.sum(share * temp, axis=0, keepdims=True)
    mean_moist = jnp.sum(share * sat, axis=0, keepdims=True)
    reply = jnp.concatenate([mean_heat, mean_moist, drift[...]], axis=0)
    reply = jnp.concatenate(halves(reply), axis=0)
    reply = jnp.concatenate(
        [reply[:, h * LANES:(h + 1) * LANES] for h in range(blocks)], axis=0).astype(BF16)
    left2 = lax.broadcasted_iota(I32, (2, LANES), 1) < HALF

    def answer(g, c):
        raw = dot(reply, near[g], NN)
        far = code_h[g]
        y = jnp.zeros((8, slots), F32)
        for h in range(blocks):
            y = y + jnp.where(far == h, raw[8 * h:8 * h + 8], 0.0)
        y = y[0:4] + y[4:8]
        for m in range(GROUP // 2):
            tile = y[:, m * LANES:(m + 1) * LANES]
            turned = pltpu.roll(tile, HALF, 1)
            send2[g * GROUP + 2 * m] = jnp.where(left2, tile[0:2], turned[2:4])
            send2[g * GROUP + 2 * m + 1] = jnp.where(left2, turned[0:2], tile[2:4])
        return c

    each_group(answer, 0)
    recv2[me] = send2[me]
    send(send2, recv2, s2, r2)
    kelvin_out = pltpu.make_async_copy(kelvin, kelvin_hbm, in_sem.at[0])
    kelvin_out.start()
    wait_all(recv2, r2)

    row = lax.broadcasted_iota(I32, (8, cols), 0) // 2
    shifted = owner8 - row

    def gather(g, acc):
        r = jnp.concatenate([recv2[g * GROUP + d] for d in range(GROUP)], axis=0)
        high, low = halves(r)
        both = jnp.concatenate([high, low], axis=1).astype(BF16)
        raw = dot(both, rout[...], NN)
        for t in range(GROUP // 4):
            m = shifted == g * GROUP + 4 * t
            acc = acc + jnp.where(jnp.concatenate([m, m], axis=1), raw[8 * t:8 * t + 8], 0.0)
        return acc

    acc = each_group(gather, jnp.zeros((8, 2 * cols), F32))
    acc = acc[0:4] + acc[4:8]
    acc = acc[0:2] + acc[2:4]
    value = jnp.concatenate([acc[:, :cols], acc[:, cols:]], axis=0)
    outs = []
    for k in reversed(range(levels)):
        value = prof[k] + fac[k] * value
        prof[k] = value
        if k % step == 0:
            rows = pl.ds(k, step)
            outs.append(pltpu.make_async_copy(
                prof.at[rows], adv_hbm.at[rows], out_sem.at[k // step]))
            outs[-1].start()
    kelvin_out.wait()
    for c in outs:
        c.wait()
    wait_all(send1, s1)
    wait_all(send2, s2)


def per_device(sizes, *args):
    gx, gy, sa = sizes
    n = gx * gy * sa
    levels, fields, cols = args[0].shape
    kinds = args[7].shape[0]
    assert n % GROUP == 0 and 2 * cols // n <= HALF and cols % LANES == 0
    groups = n // GROUP
    pieces = 4 if levels % 4 == 0 else 1
    vmem = [pltpu.VMEM(a.shape, a.dtype) for a in args]
    return pl.pallas_call(
        functools.partial(kernel, (gx, gy, sa, levels, cols, pieces)),
        out_shape=(
            jax.ShapeDtypeStruct(args[0].shape, F32),
            jax.ShapeDtypeStruct((kinds, cols), F32),
        ),
        in_specs=[pl.BlockSpec(memory_space=pl.ANY)] * len(args),
        out_specs=[pl.BlockSpec(memory_space=pl.ANY)] * 2,
        scratch_shapes=vmem + [
            pltpu.VMEM(args[0].shape, F32),
            pltpu.VMEM((kinds, cols), F32),
            pltpu.VMEM((2 * LANES, 2 * cols), BF16),
            pltpu.VMEM((8 * GROUP, 2 * cols), BF16),
            pltpu.VMEM((groups, LANES, GROUP * HALF), BF16),
            pltpu.VMEM((groups, 8, GROUP * HALF), I32),
            pltpu.VMEM((n, 4, LANES), F32),
            pltpu.VMEM((n, 4, LANES), F32),
            pltpu.VMEM((n, 2, LANES), F32),
            pltpu.VMEM((n, 2, LANES), F32),
            pltpu.SemaphoreType.DMA((7,)),
            pltpu.SemaphoreType.DMA((2, pieces)),
            pltpu.SemaphoreType.DMA((pieces,)),
            pltpu.SemaphoreType.DMA,
            pltpu.SemaphoreType.DMA,
            pltpu.SemaphoreType.DMA,
            pltpu.SemaphoreType.DMA,
        ],
        compiler_params=pltpu.CompilerParams(collective_id=0, has_side_effects=True),
    )(*args)


def solution(mesh):
    wide = P(None, None, AXES)
    flat = P(None, AXES)
    return jax.shard_map(
        functools.partial(per_device, tuple(mesh.shape[a] for a in AXES)),
        mesh=mesh,
        in_specs=(wide, wide) + (flat,) * 7,
        out_specs=(wide, flat),
        check_vma=False,
    )
```

```python
import functools

import jax
import jax.numpy as jnp
from jax import lax
from jax.experimental import pallas as pl
from jax.experimental.pallas import tpu as pltpu
from jax.sharding import PartitionSpec as P

SWEEPS = 3
AXES = ("gx", "gy", "sa")
LANES = 128
HALF = LANES // 2
GROUP = 32
F32, BF16, I32 = jnp.float32, jnp.bfloat16, jnp.int32
VMEM_GRANT = 32 * 1024 * 1024
NT = (((1,), (1,)), ((), ()))
NN = (((1,), (0,)), ((), ()))


def dot(a, b, dims):
    return lax.dot_general(a, b, dims, preferred_element_type=F32)


def halves(x):
    high = x.astype(BF16).astype(F32)
    return high, x - high


def one_hot(mask):
    return jnp.where(mask, 1.0, 0.0).astype(BF16)


def kernel(
    sizes,
    prof_hbm, turb_hbm, owner_hbm, frac_hbm, flag_hbm, flux_hbm, link_hbm, base_hbm, drift_hbm,
    off_all, fac, boundary, kelvin,
    prof, turb, owner_v, frac, flag, flux, link, base, drift,
    rout, lhs, near, code_h, send1, recv1, send2, recv2,
    in_sem, lev_sem, s1, r1, s2, r2,
):
    gx, gy, sa, levels, cols, pieces = sizes
    n = gx * gy * sa
    blocks = cols // LANES
    groups = n // GROUP
    step = levels // pieces
    me = (lax.axis_index("gx") * gy + lax.axis_index("gy")) * sa + lax.axis_index("sa")

    def peer(o):
        q = me + o
        return jnp.where(q >= n, q - n, q)

    def peers(fn):
        if n <= GROUP:
            for o in range(1, n):
                fn(o)
        else:
            def body(o, c):
                fn(o)
                return c
            lax.fori_loop(1, n, body, 0)

    def each_group(fn, init):
        if groups == 1:
            return fn(0, init)
        return lax.fori_loop(0, groups, fn, init)

    loads = [
        pltpu.make_async_copy(a, b, in_sem.at[i])
        for i, (a, b) in enumerate((
            (owner_hbm, owner_v), (frac_hbm, frac), (flag_hbm, flag), (flux_hbm, flux),
            (link_hbm, link), (base_hbm, base), (drift_hbm, drift)))
    ]
    loads[0].start()
    lev_loads = []
    for i in range(pieces):
        rows = pl.ds(i * step, step)
        lev_loads.append((
            pltpu.make_async_copy(turb_hbm.at[rows], turb.at[rows], lev_sem.at[0, i]),
            pltpu.make_async_copy(prof_hbm.at[rows], prof.at[rows], lev_sem.at[1, i])))
        for c in lev_loads[-1]:
            c.start()
    for c in loads[1:]:
        c.start()

    barrier = pltpu.get_barrier_semaphore()
    peers(lambda o: pl.semaphore_signal(
        barrier, inc=1, device_id=peer(o), device_id_type=pl.DeviceIdType.LOGICAL))

    loads[0].wait()
    owner = owner_v[0:1, :]
    local = owner_v[1:2, :]
    onehot_d = lax.broadcasted_iota(I32, (n, cols), 0) == owner
    d01 = one_hot(onehot_d)
    stacked = jnp.concatenate([d01[:, b * LANES:(b + 1) * LANES] for b in range(blocks)], axis=0)
    ti = lax.broadcasted_iota(I32, (LANES, 2 * LANES), 0)
    tj = lax.broadcasted_iota(I32, (LANES, 2 * LANES), 1)
    tri = one_hot((ti < tj) | (tj >= LANES))
    counts = dot(stacked, tri, NN)
    carry = jnp.zeros((n, LANES), F32)
    ranks = []
    for b in range(blocks):
        part = counts[b * n:(b + 1) * n]
        mask = onehot_d[:, b * LANES:(b + 1) * LANES]
        ranks.append(jnp.sum(jnp.where(mask, part[:, :LANES] + carry, 0.0), axis=0, keepdims=True))
        carry = carry + part[:, LANES:]
    rank = jnp.concatenate(ranks, axis=1).astype(I32)
    r01 = one_hot(lax.broadcasted_iota(I32, (HALF, cols), 0) == rank)
    zero = jnp.zeros((HALF, cols), BF16)
    for i in range(2):
        rout[pl.ds(i * LANES, HALF), 0:cols] = r01
        rout[pl.ds(i * LANES, HALF), cols:2 * cols] = zero
        rout[pl.ds(i * LANES + HALF, HALF), 0:cols] = zero
        rout[pl.ds(i * LANES + HALF, HALF), cols:2 * cols] = r01

    def eliminate(row, v, wait):
        above = off = factor = None
        for k in range(levels):
            if wait and k % step == 0:
                for c in lev_loads[k // step]:
                    c.wait()
            below = jnp.broadcast_to(turb[k, row:row + 1, :], (2, cols))
            x = prof[k, v:v + 2, :]
            if k == 0:
                inv = 1.0 / (1.0 + below)
                off = x * inv
            else:
                inv = 1.0 / (1.0 + above * (1.0 - factor) + below)
                off = (x + above * off) * inv
            factor = below * inv
            above = below
            off_all[k, v:v + 2, :] = off
            fac[k, v:v + 2, :] = factor
        return off, factor, below

    off, factor, below = eliminate(0, 0, True)
    code = (local + 1).astype(F32)
    blank = jnp.zeros_like(code)
    even = jnp.concatenate([off[0:1], factor[0:1], code, blank], axis=0)
    odd = jnp.concatenate([off[1:2], below[1:2], code, blank], axis=0)
    wide = jnp.concatenate([
        jnp.concatenate(halves(even), axis=0), jnp.concatenate(halves(odd), axis=0)], axis=1)
    owner8 = jnp.broadcast_to(owner, (8, cols))

    def dispatch(g, c):
        for t in range(GROUP // 2):
            parts = []
            for u in range(2):
                m = owner8 == g * GROUP + 2 * t + u
                parts.append(jnp.where(jnp.concatenate([m, m], axis=1), wide, 0.0))
            lhs[pl.ds(16 * t, 16), :] = jnp.concatenate(parts, axis=0).astype(BF16)
        out = dot(lhs[...], rout[0:LANES, :], NT)
        for d in range(GROUP):
            send1[g * GROUP + d] = out[8 * d:8 * d + 4] + out[8 * d + 4:8 * d + 8]
        return c

    each_group(dispatch, 0)
    recv1[me] = send1[me]

    pl.semaphore_wait(barrier, n - 1)

    def send(src, dst, ss, rs):
        def one(o):
            q = peer(o)
            pltpu.make_async_remote_copy(
                src_ref=src.at[q], dst_ref=dst.at[me], send_sem=ss, recv_sem=rs,
                device_id=q, device_id_type=pl.DeviceIdType.LOGICAL).start()
        peers(one)

    def wait_all(buf, sem):
        part = buf.at[pl.ds(0, n - 1)]
        pltpu.make_async_copy(part, part, sem).wait()

    send(send1, recv1, s1, r1)

    eliminate(1, 2, False)
    for c in loads[1:]:
        c.wait()
    present = jnp.concatenate(
        [jnp.ones((1, cols), F32), flag[...].astype(F32)], axis=0)
    share = frac[...] * present
    share = share / jnp.sum(share, axis=0, keepdims=True)

    wait_all(recv1, r1)
    lane = lax.broadcasted_iota(I32, (4, LANES), 1)
    left = lane < HALF
    slots = GROUP * HALF

    def collect(g, acc):
        evens, odds = [], []
        for m in range(GROUP // 2):
            a = recv1[g * GROUP + 2 * m]
            b = recv1[g * GROUP + 2 * m + 1]
            evens.append(jnp.where(left, a, pltpu.roll(b, HALF, 1)))
            odds.append(jnp.where(left, pltpu.roll(a, HALF, 1), b))
        even = jnp.concatenate(evens, axis=1)
        odd = jnp.concatenate(odds, axis=1)
        at = even[2:3].astype(I32) - 1
        high, low = halves(jnp.concatenate([even[0:2], odd[0:2]], axis=0))
        v = jnp.concatenate([high, low], axis=0)
        at8 = jnp.broadcast_to(at, (8, slots))
        far = at8 // LANES
        far = jnp.where(at8 < 0, -1, far)
        code_h[g] = far
        within = at - far[0:1] * LANES
        jl = one_hot(lax.broadcasted_iota(I32, (LANES, slots), 0) == within)
        near[g] = jl
        rows = jnp.concatenate(
            [jnp.where(far == h, v, 0.0) for h in range(blocks)], axis=0).astype(BF16)
        return acc + dot(rows, jl, NT)

    got = each_group(collect, jnp.zeros((8 * blocks, LANES), F32))
    x = jnp.concatenate(
        [got[8 * h:8 * h + 4] + got[8 * h + 4:8 * h + 8] for h in range(blocks)], axis=1)
    kinds = base.shape[0]
    off_h, fac_s, off_m, exch = [jnp.broadcast_to(x[i:i + 1], (kinds, cols)) for i in range(4)]
    bottom = base[...]
    absorbed = flux[...]
    coupled = link[...]
    temp = bottom
    for _ in range(SWEEPS):
        sat = 0.6 * jnp.exp(0.3 * temp)
        mean_heat = jnp.sum(share * temp, axis=0, keepdims=True)
        mean_moist = jnp.sum(share * sat, axis=0, keepdims=True)
        air_heat = off_h + fac_s * mean_heat
        air_moist = off_m + fac_s * mean_moist
        emitted = 0.5 * jnp.exp(0.2 * temp)
        imbalance = (absorbed - emitted - exch * (temp - air_heat)
                     - 2.5 * exch * (sat - air_moist) - coupled * (temp - bottom))
        slope = 0.2 * emitted + exch * (1.0 + 2.5 * 0.3 * sat) + coupled
        temp = temp + imbalance / slope
    kelvin[...] = temp
    sat = 0.6 * jnp.exp(0.3 * temp)
    mean_heat = jnp.sum(share * temp, axis=0, keepdims=True)
    mean_moist = jnp.sum(share * sat, axis=0, keepdims=True)
    reply = jnp.concatenate([mean_heat, mean_moist, drift[...]], axis=0)
    reply = jnp.concatenate(halves(reply), axis=0)
    reply = jnp.concatenate(
        [reply[:, h * LANES:(h + 1) * LANES] for h in range(blocks)], axis=0).astype(BF16)
    left2 = lax.broadcasted_iota(I32, (2, LANES), 1) < HALF

    def answer(g, c):
        raw = dot(reply, near[g], NN)
        far = code_h[g]
        y = jnp.zeros((8, slots), F32)
        for h in range(blocks):
            y = y + jnp.where(far == h, raw[8 * h:8 * h + 8], 0.0)
        y = y[0:4] + y[4:8]
        for m in range(GROUP // 2):
            tile = y[:, m * LANES:(m + 1) * LANES]
            turned = pltpu.roll(tile, HALF, 1)
            send2[g * GROUP + 2 * m] = jnp.where(left2, tile[0:2], turned[2:4])
            send2[g * GROUP + 2 * m + 1] = jnp.where(left2, turned[0:2], tile[2:4])
        return c

    each_group(answer, 0)
    recv2[me] = send2[me]
    send(send2, recv2, s2, r2)
    wait_all(recv2, r2)

    row = lax.broadcasted_iota(I32, (8, cols), 0) // 2
    shifted = owner8 - row

    def gather(g, acc):
        r = jnp.concatenate([recv2[g * GROUP + d] for d in range(GROUP)], axis=0)
        high, low = halves(r)
        both = jnp.concatenate([high, low], axis=1).astype(BF16)
        raw = dot(both, rout[...], NN)
        for t in range(GROUP // 4):
            m = shifted == g * GROUP + 4 * t
            acc = acc + jnp.where(jnp.concatenate([m, m], axis=1), raw[8 * t:8 * t + 8], 0.0)
        return acc

    acc = each_group(gather, jnp.zeros((8, 2 * cols), F32))
    acc = acc[0:4] + acc[4:8]
    acc = acc[0:2] + acc[2:4]
    boundary[...] = jnp.concatenate([acc[:, :cols], acc[:, cols:]], axis=0)
    wait_all(send1, s1)
    wait_all(send2, s2)


def finish(pieces, off, fac, boundary, kelvin, adv_hbm, kelvin_hbm, adv, out_sem, kelvin_sem):
    levels = off.shape[0]
    step = levels // pieces
    kelvin_out = pltpu.make_async_copy(kelvin, kelvin_hbm, kelvin_sem)
    kelvin_out.start()
    value = boundary[...]
    outs = []
    for k in reversed(range(levels)):
        value = off[k] + fac[k] * value
        adv[k] = value
        if k % step == 0:
            rows = pl.ds(k, step)
            outs.append(pltpu.make_async_copy(
                adv.at[rows], adv_hbm.at[rows], out_sem.at[k // step]))
            outs[-1].start()
    kelvin_out.wait()
    for c in outs:
        c.wait()


def per_device(sizes, *args):
    gx, gy, sa = sizes
    n = gx * gy * sa
    levels, fields, cols = args[0].shape
    kinds = args[7].shape[0]
    assert n % GROUP == 0 and 2 * cols // n <= HALF and cols % LANES == 0
    groups = n // GROUP
    pieces = 4 if levels % 4 == 0 else 1
    vmem = [pltpu.VMEM(a.shape, a.dtype) for a in args]
    off, fac, boundary, kelvin = pl.pallas_call(
        functools.partial(kernel, (gx, gy, sa, levels, cols, pieces)),
        out_shape=(
            pltpu.VMEM(args[0].shape, F32),
            pltpu.VMEM(args[0].shape, F32),
            pltpu.VMEM((fields, cols), F32),
            pltpu.VMEM((kinds, cols), F32),
        ),
        in_specs=[pl.BlockSpec(memory_space=pltpu.HBM)] * len(args),
        out_specs=[pl.BlockSpec(memory_space=pltpu.VMEM)] * 4,
        scratch_shapes=vmem + [
            pltpu.VMEM((2 * LANES, 2 * cols), BF16),
            pltpu.VMEM((8 * GROUP, 2 * cols), BF16),
            pltpu.VMEM((groups, LANES, GROUP * HALF), BF16),
            pltpu.VMEM((groups, 8, GROUP * HALF), I32),
            pltpu.VMEM((n, 4, LANES), F32),
            pltpu.VMEM((n, 4, LANES), F32),
            pltpu.VMEM((n, 2, LANES), F32),
            pltpu.VMEM((n, 2, LANES), F32),
            pltpu.SemaphoreType.DMA((7,)),
            pltpu.SemaphoreType.DMA((2, pieces)),
            pltpu.SemaphoreType.DMA,
            pltpu.SemaphoreType.DMA,
            pltpu.SemaphoreType.DMA,
            pltpu.SemaphoreType.DMA,
        ],
        compiler_params=pltpu.CompilerParams(
            collective_id=0, has_side_effects=True, vmem_limit_bytes=VMEM_GRANT),
    )(*args)
    return pl.pallas_call(
        functools.partial(finish, pieces),
        out_shape=(
            jax.ShapeDtypeStruct(args[0].shape, F32),
            jax.ShapeDtypeStruct((kinds, cols), F32),
        ),
        in_specs=[pl.BlockSpec(memory_space=pltpu.VMEM)] * 4,
        out_specs=[pl.BlockSpec(memory_space=pltpu.HBM)] * 2,
        scratch_shapes=[
            pltpu.VMEM(args[0].shape, F32),
            pltpu.SemaphoreType.DMA((pieces,)),
            pltpu.SemaphoreType.DMA,
        ],
        compiler_params=pltpu.CompilerParams(vmem_limit_bytes=VMEM_GRANT),
    )(off, fac, boundary, kelvin)


def solution(mesh):
    wide = P(None, None, AXES)
    flat = P(None, AXES)
    return jax.shard_map(
        functools.partial(per_device, tuple(mesh.shape[a] for a in AXES)),
        mesh=mesh,
        in_specs=(wide, wide) + (flat,) * 7,
        out_specs=(wide, flat),
        check_vma=False,
    )
```

```python
import functools

import jax
import jax.numpy as jnp
from jax import lax
from jax.experimental import pallas as pl
from jax.experimental.pallas import tpu as pltpu
from jax.sharding import PartitionSpec as P

SWEEPS = 3
AXES = ("gx", "gy", "sa")
LANES = 128
HALF = LANES // 2
GROUP = 32
F32, BF16, I32 = jnp.float32, jnp.bfloat16, jnp.int32
VMEM_GRANT = 60 * 1024 * 1024
FINISH_GRANT = 4 * 1024 * 1024
NT = (((1,), (1,)), ((), ()))
NN = (((1,), (0,)), ((), ()))


def dot(a, b, dims):
    return lax.dot_general(a, b, dims, preferred_element_type=F32)


def halves(x):
    high = x.astype(BF16).astype(F32)
    return high, x - high


def one_hot(mask):
    return jnp.where(mask, 1.0, 0.0).astype(BF16)


def kernel(
    sizes,
    prof_hbm, turb_hbm, owner_hbm, frac_hbm, flag_hbm, flux_hbm, link_hbm, base_hbm, drift_hbm,
    off_all, fac, boundary, kelvin,
    prof, turb, owner_v, frac, flag, flux, link, base, drift,
    rout, lhs, near, code_h, send1, recv1, send2, recv2,
    in_sem, lev_sem, s1, r1, s2, r2,
):
    gx, gy, sa, levels, cols, pieces = sizes
    n = gx * gy * sa
    blocks = cols // LANES
    groups = n // GROUP
    step = levels // pieces
    me = (lax.axis_index("gx") * gy + lax.axis_index("gy")) * sa + lax.axis_index("sa")

    def peer(o):
        q = me + o
        return jnp.where(q >= n, q - n, q)

    def peers(fn):
        if n <= GROUP:
            for o in range(1, n):
                fn(o)
        else:
            def body(o, c):
                fn(o)
                return c
            lax.fori_loop(1, n, body, 0)

    def each_group(fn, init):
        if groups == 1:
            return fn(0, init)
        return lax.fori_loop(0, groups, fn, init)

    loads = [
        pltpu.make_async_copy(a, b, in_sem.at[i])
        for i, (a, b) in enumerate((
            (owner_hbm, owner_v), (frac_hbm, frac), (flag_hbm, flag), (flux_hbm, flux),
            (link_hbm, link), (base_hbm, base), (drift_hbm, drift)))
    ]
    loads[0].start()
    lev_loads = []
    for i in range(pieces):
        rows = pl.ds(i * step, step)
        lev_loads.append((
            pltpu.make_async_copy(turb_hbm.at[rows], turb.at[rows], lev_sem.at[0, i]),
            pltpu.make_async_copy(prof_hbm.at[rows], prof.at[rows], lev_sem.at[1, i])))
        for c in lev_loads[-1]:
            c.start()
    for c in loads[1:]:
        c.start()

    barrier = pltpu.get_barrier_semaphore()
    peers(lambda o: pl.semaphore_signal(
        barrier, inc=1, device_id=peer(o), device_id_type=pl.DeviceIdType.LOGICAL))

    loads[0].wait()
    owner = owner_v[0:1, :]
    local = owner_v[1:2, :]
    onehot_d = lax.broadcasted_iota(I32, (n, cols), 0) == owner
    d01 = one_hot(onehot_d)
    stacked = jnp.concatenate([d01[:, b * LANES:(b + 1) * LANES] for b in range(blocks)], axis=0)
    ti = lax.broadcasted_iota(I32, (LANES, 2 * LANES), 0)
    tj = lax.broadcasted_iota(I32, (LANES, 2 * LANES), 1)
    tri = one_hot((ti < tj) | (tj >= LANES))
    counts = dot(stacked, tri, NN)
    carry = jnp.zeros((n, LANES), F32)
    ranks = []
    for b in range(blocks):
        part = counts[b * n:(b + 1) * n]
        mask = onehot_d[:, b * LANES:(b + 1) * LANES]
        ranks.append(jnp.sum(jnp.where(mask, part[:, :LANES] + carry, 0.0), axis=0, keepdims=True))
        carry = carry + part[:, LANES:]
    rank = jnp.concatenate(ranks, axis=1).astype(I32)
    r01 = one_hot(lax.broadcasted_iota(I32, (HALF, cols), 0) == rank)
    zero = jnp.zeros((HALF, cols), BF16)
    for i in range(2):
        rout[pl.ds(i * LANES, HALF), 0:cols] = r01
        rout[pl.ds(i * LANES, HALF), cols:2 * cols] = zero
        rout[pl.ds(i * LANES + HALF, HALF), 0:cols] = zero
        rout[pl.ds(i * LANES + HALF, HALF), cols:2 * cols] = r01

    def eliminate(row, v, wait):
        above = off = factor = None
        for k in range(levels):
            if wait and k % step == 0:
                for c in lev_loads[k // step]:
                    c.wait()
            below = jnp.broadcast_to(turb[k, row:row + 1, :], (2, cols))
            x = prof[k, v:v + 2, :]
            if k == 0:
                inv = 1.0 / (1.0 + below)
                off = x * inv
            else:
                inv = 1.0 / (1.0 + above * (1.0 - factor) + below)
                off = (x + above * off) * inv
            factor = below * inv
            above = below
            off_all[k, v:v + 2, :] = off
            fac[k, v:v + 2, :] = factor
        return off, factor, below

    off, factor, below = eliminate(0, 0, True)
    code = (local + 1).astype(F32)
    blank = jnp.zeros_like(code)
    even = jnp.concatenate([off[0:1], factor[0:1], code, blank], axis=0)
    odd = jnp.concatenate([off[1:2], below[1:2], code, blank], axis=0)
    wide = jnp.concatenate([
        jnp.concatenate(halves(even), axis=0), jnp.concatenate(halves(odd), axis=0)], axis=1)
    owner8 = jnp.broadcast_to(owner, (8, cols))

    def dispatch(g, c):
        for t in range(GROUP // 2):
            parts = []
            for u in range(2):
                m = owner8 == g * GROUP + 2 * t + u
                parts.append(jnp.where(jnp.concatenate([m, m], axis=1), wide, 0.0))
            lhs[pl.ds(16 * t, 16), :] = jnp.concatenate(parts, axis=0).astype(BF16)
        out = dot(lhs[...], rout[0:LANES, :], NT)
        for d in range(GROUP):
            send1[g * GROUP + d] = out[8 * d:8 * d + 4] + out[8 * d + 4:8 * d + 8]
        return c

    each_group(dispatch, 0)
    recv1[me] = send1[me]

    pl.semaphore_wait(barrier, n - 1)

    def send(src, dst, ss, rs):
        def one(o):
            q = peer(o)
            pltpu.make_async_remote_copy(
                src_ref=src.at[q], dst_ref=dst.at[me], send_sem=ss, recv_sem=rs,
                device_id=q, device_id_type=pl.DeviceIdType.LOGICAL).start()
        peers(one)

    def wait_all(buf, sem):
        part = buf.at[pl.ds(0, n - 1)]
        pltpu.make_async_copy(part, part, sem).wait()

    send(send1, recv1, s1, r1)

    eliminate(1, 2, False)
    for c in loads[1:]:
        c.wait()
    present = jnp.concatenate(
        [jnp.ones((1, cols), F32), flag[...].astype(F32)], axis=0)
    share = frac[...] * present
    share = share / jnp.sum(share, axis=0, keepdims=True)

    wait_all(recv1, r1)
    lane = lax.broadcasted_iota(I32, (4, LANES), 1)
    left = lane < HALF
    slots = GROUP * HALF

    def collect(g, acc):
        evens, odds = [], []
        for m in range(GROUP // 2):
            a = recv1[g * GROUP + 2 * m]
            b = recv1[g * GROUP + 2 * m + 1]
            evens.append(jnp.where(left, a, pltpu.roll(b, HALF, 1)))
            odds.append(jnp.where(left, pltpu.roll(a, HALF, 1), b))
        even = jnp.concatenate(evens, axis=1)
        odd = jnp.concatenate(odds, axis=1)
        at = even[2:3].astype(I32) - 1
        high, low = halves(jnp.concatenate([even[0:2], odd[0:2]], axis=0))
        v = jnp.concatenate([high, low], axis=0)
        at8 = jnp.broadcast_to(at, (8, slots))
        far = at8 // LANES
        far = jnp.where(at8 < 0, -1, far)
        code_h[g] = far
        within = at - far[0:1] * LANES
        jl = one_hot(lax.broadcasted_iota(I32, (LANES, slots), 0) == within)
        near[g] = jl
        rows = jnp.concatenate(
            [jnp.where(far == h, v, 0.0) for h in range(blocks)], axis=0).astype(BF16)
        return acc + dot(rows, jl, NT)

    got = each_group(collect, jnp.zeros((8 * blocks, LANES), F32))
    x = jnp.concatenate(
        [got[8 * h:8 * h + 4] + got[8 * h + 4:8 * h + 8] for h in range(blocks)], axis=1)
    kinds = base.shape[0]
    off_h, fac_s, off_m, exch = [jnp.broadcast_to(x[i:i + 1], (kinds, cols)) for i in range(4)]
    bottom = base[...]
    absorbed = flux[...]
    coupled = link[...]
    temp = bottom
    for _ in range(SWEEPS):
        sat = 0.6 * jnp.exp(0.3 * temp)
        mean_heat = jnp.sum(share * temp, axis=0, keepdims=True)
        mean_moist = jnp.sum(share * sat, axis=0, keepdims=True)
        air_heat = off_h + fac_s * mean_heat
        air_moist = off_m + fac_s * mean_moist
        emitted = 0.5 * jnp.exp(0.2 * temp)
        imbalance = (absorbed - emitted - exch * (temp - air_heat)
                     - 2.5 * exch * (sat - air_moist) - coupled * (temp - bottom))
        slope = 0.2 * emitted + exch * (1.0 + 2.5 * 0.3 * sat) + coupled
        temp = temp + imbalance / slope
    kelvin[...] = temp
    sat = 0.6 * jnp.exp(0.3 * temp)
    mean_heat = jnp.sum(share * temp, axis=0, keepdims=True)
    mean_moist = jnp.sum(share * sat, axis=0, keepdims=True)
    reply = jnp.concatenate([mean_heat, mean_moist, drift[...]], axis=0)
    reply = jnp.concatenate(halves(reply), axis=0)
    reply = jnp.concatenate(
        [reply[:, h * LANES:(h + 1) * LANES] for h in range(blocks)], axis=0).astype(BF16)
    left2 = lax.broadcasted_iota(I32, (2, LANES), 1) < HALF

    def answer(g, c):
        raw = dot(reply, near[g], NN)
        far = code_h[g]
        y = jnp.zeros((8, slots), F32)
        for h in range(blocks):
            y = y + jnp.where(far == h, raw[8 * h:8 * h + 8], 0.0)
        y = y[0:4] + y[4:8]
        for m in range(GROUP // 2):
            tile = y[:, m * LANES:(m + 1) * LANES]
            turned = pltpu.roll(tile, HALF, 1)
            send2[g * GROUP + 2 * m] = jnp.where(left2, tile[0:2], turned[2:4])
            send2[g * GROUP + 2 * m + 1] = jnp.where(left2, turned[0:2], tile[2:4])
        return c

    each_group(answer, 0)
    recv2[me] = send2[me]
    send(send2, recv2, s2, r2)
    wait_all(recv2, r2)

    row = lax.broadcasted_iota(I32, (8, cols), 0) // 2
    shifted = owner8 - row

    def gather(g, acc):
        r = jnp.concatenate([recv2[g * GROUP + d] for d in range(GROUP)], axis=0)
        high, low = halves(r)
        both = jnp.concatenate([high, low], axis=1).astype(BF16)
        raw = dot(both, rout[...], NN)
        for t in range(GROUP // 4):
            m = shifted == g * GROUP + 4 * t
            acc = acc + jnp.where(jnp.concatenate([m, m], axis=1), raw[8 * t:8 * t + 8], 0.0)
        return acc

    acc = each_group(gather, jnp.zeros((8, 2 * cols), F32))
    acc = acc[0:4] + acc[4:8]
    acc = acc[0:2] + acc[2:4]
    boundary[...] = jnp.concatenate([acc[:, :cols], acc[:, cols:]], axis=0)
    wait_all(send1, s1)
    wait_all(send2, s2)


def finish(pieces, off, fac, boundary, kelvin, adv_hbm, kelvin_hbm, adv, out_sem, kelvin_sem):
    levels = off.shape[0]
    step = levels // pieces
    kelvin_out = pltpu.make_async_copy(kelvin, kelvin_hbm, kelvin_sem)
    kelvin_out.start()
    value = boundary[...]
    outs = []
    for k in reversed(range(levels)):
        value = off[k] + fac[k] * value
        adv[k] = value
        if k % step == 0:
            rows = pl.ds(k, step)
            outs.append(pltpu.make_async_copy(
                adv.at[rows], adv_hbm.at[rows], out_sem.at[k // step]))
            outs[-1].start()
    kelvin_out.wait()
    for c in outs:
        c.wait()


def per_device(sizes, *args):
    gx, gy, sa = sizes
    n = gx * gy * sa
    levels, fields, cols = args[0].shape
    kinds = args[7].shape[0]
    assert n % GROUP == 0 and 2 * cols // n <= HALF and cols % LANES == 0
    groups = n // GROUP
    pieces = 4 if levels % 4 == 0 else 1
    vmem = [pltpu.VMEM(a.shape, a.dtype) for a in args]
    off, fac, boundary, kelvin = pl.pallas_call(
        functools.partial(kernel, (gx, gy, sa, levels, cols, pieces)),
        out_shape=(
            pltpu.VMEM(args[0].shape, F32),
            pltpu.VMEM(args[0].shape, F32),
            pltpu.VMEM((fields, cols), F32),
            pltpu.VMEM((kinds, cols), F32),
        ),
        in_specs=[pl.BlockSpec(memory_space=pltpu.HBM)] * len(args),
        out_specs=[pl.BlockSpec(memory_space=pltpu.VMEM)] * 4,
        scratch_shapes=vmem + [
            pltpu.VMEM((2 * LANES, 2 * cols), BF16),
            pltpu.VMEM((8 * GROUP, 2 * cols), BF16),
            pltpu.VMEM((groups, LANES, GROUP * HALF), BF16),
            pltpu.VMEM((groups, 8, GROUP * HALF), I32),
            pltpu.VMEM((n, 4, LANES), F32),
            pltpu.VMEM((n, 4, LANES), F32),
            pltpu.VMEM((n, 2, LANES), F32),
            pltpu.VMEM((n, 2, LANES), F32),
            pltpu.SemaphoreType.DMA((7,)),
            pltpu.SemaphoreType.DMA((2, pieces)),
            pltpu.SemaphoreType.DMA,
            pltpu.SemaphoreType.DMA,
            pltpu.SemaphoreType.DMA,
            pltpu.SemaphoreType.DMA,
        ],
        compiler_params=pltpu.CompilerParams(
            collective_id=0, has_side_effects=True, vmem_limit_bytes=VMEM_GRANT),
    )(*args)
    return pl.pallas_call(
        functools.partial(finish, pieces),
        out_shape=(
            jax.ShapeDtypeStruct(args[0].shape, F32),
            jax.ShapeDtypeStruct((kinds, cols), F32),
        ),
        in_specs=[pl.BlockSpec(memory_space=pltpu.VMEM)] * 4,
        out_specs=[pl.BlockSpec(memory_space=pltpu.HBM)] * 2,
        scratch_shapes=[
            pltpu.VMEM(args[0].shape, F32),
            pltpu.SemaphoreType.DMA((pieces,)),
            pltpu.SemaphoreType.DMA,
        ],
        compiler_params=pltpu.CompilerParams(vmem_limit_bytes=FINISH_GRANT),
    )(off, fac, boundary, kelvin)


def solution(mesh):
    wide = P(None, None, AXES)
    flat = P(None, AXES)
    return jax.shard_map(
        functools.partial(per_device, tuple(mesh.shape[a] for a in AXES)),
        mesh=mesh,
        in_specs=(wide, wide) + (flat,) * 7,
        out_specs=(wide, flat),
        check_vma=False,
    )
```

```python
import functools

import jax
import jax.numpy as jnp
from jax import lax
from jax.experimental import pallas as pl
from jax.experimental.pallas import tpu as pltpu
from jax.sharding import PartitionSpec as P

SWEEPS = 3
AXES = ("gx", "gy", "sa")
LANES = 128
HALF = LANES // 2
GROUP = 32
F32, BF16, I32 = jnp.float32, jnp.bfloat16, jnp.int32
VMEM_GRANT = 60 * 1024 * 1024
FINISH_GRANT = 4 * 1024 * 1024
NT = (((1,), (1,)), ((), ()))
NN = (((1,), (0,)), ((), ()))


def dot(a, b, dims):
    return lax.dot_general(a, b, dims, preferred_element_type=F32)


def halves(x):
    high = x.astype(BF16).astype(F32)
    return high, x - high


def one_hot(mask):
    return jnp.where(mask, 1.0, 0.0).astype(BF16)


def kernel(
    sizes,
    prof_hbm, turb_hbm, owner_hbm, frac_hbm, flag_hbm, flux_hbm, link_hbm, base_hbm, drift_hbm,
    off_all, fac, boundary, kelvin,
    prof, turb, owner_v, frac, flag, flux, link, base, drift,
    rout, lhs, near, code_h, send1, recv1, send2, recv2,
    in_sem, lev_sem, s1, r1, s2, r2,
):
    gx, gy, sa, levels, cols, pieces = sizes
    n = gx * gy * sa
    blocks = cols // LANES
    groups = n // GROUP
    step = levels // pieces
    me = (lax.axis_index("gx") * gy + lax.axis_index("gy")) * sa + lax.axis_index("sa")

    mine = lax.axis_index("gx")
    upper = 2 * mine >= gx
    crew = n // gx

    def peer(t):
        q = jnp.where(upper, t, n - 2 - t)
        return q + jnp.where(q >= me, 1, 0)

    def peers(fn):
        if n <= GROUP:
            for o in range(n - 1):
                fn(o)
        else:
            def body(o, c):
                fn(o)
                return c
            lax.fori_loop(0, n - 1, body, 0)

    def each(count, fn, init):
        if count > 4:
            return lax.fori_loop(0, count, fn, init)
        for i in range(count):
            init = fn(i, init)
        return init

    def crew_at(i):
        return jnp.where(upper, gx - 1 - i, i)

    loads = [
        pltpu.make_async_copy(a, b, in_sem.at[i])
        for i, (a, b) in enumerate((
            (owner_hbm, owner_v), (frac_hbm, frac), (flag_hbm, flag), (flux_hbm, flux),
            (link_hbm, link), (base_hbm, base), (drift_hbm, drift)))
    ]
    loads[0].start()
    lev_loads = []
    for i in range(pieces):
        rows = pl.ds(i * step, step)
        lev_loads.append((
            pltpu.make_async_copy(turb_hbm.at[rows], turb.at[rows], lev_sem.at[0, i]),
            pltpu.make_async_copy(prof_hbm.at[rows], prof.at[rows], lev_sem.at[1, i])))
        for c in lev_loads[-1]:
            c.start()
    for c in loads[1:]:
        c.start()

    barrier = pltpu.get_barrier_semaphore()
    peers(lambda o: pl.semaphore_signal(
        barrier, inc=1, device_id=peer(o), device_id_type=pl.DeviceIdType.LOGICAL))

    loads[0].wait()
    owner = owner_v[0:1, :]
    local = owner_v[1:2, :]
    onehot_d = lax.broadcasted_iota(I32, (n, cols), 0) == owner
    d01 = one_hot(onehot_d)
    stacked = jnp.concatenate([d01[:, b * LANES:(b + 1) * LANES] for b in range(blocks)], axis=0)
    ti = lax.broadcasted_iota(I32, (LANES, 2 * LANES), 0)
    tj = lax.broadcasted_iota(I32, (LANES, 2 * LANES), 1)
    tri = one_hot((ti < tj) | (tj >= LANES))
    counts = dot(stacked, tri, NN)
    carry = jnp.zeros((n, LANES), F32)
    ranks = []
    for b in range(blocks):
        part = counts[b * n:(b + 1) * n]
        mask = onehot_d[:, b * LANES:(b + 1) * LANES]
        ranks.append(jnp.sum(jnp.where(mask, part[:, :LANES] + carry, 0.0), axis=0, keepdims=True))
        carry = carry + part[:, LANES:]
    rank = jnp.concatenate(ranks, axis=1).astype(I32)
    r01 = one_hot(lax.broadcasted_iota(I32, (HALF, cols), 0) == rank)
    zero = jnp.zeros((HALF, cols), BF16)
    for i in range(2):
        rout[pl.ds(i * LANES, HALF), 0:cols] = r01
        rout[pl.ds(i * LANES, HALF), cols:2 * cols] = zero
        rout[pl.ds(i * LANES + HALF, HALF), 0:cols] = zero
        rout[pl.ds(i * LANES + HALF, HALF), cols:2 * cols] = r01

    def eliminate(row, v, wait):
        above = off = factor = None
        for k in range(levels):
            if wait and k % step == 0:
                for c in lev_loads[k // step]:
                    c.wait()
            below = jnp.broadcast_to(turb[k, row:row + 1, :], (2, cols))
            x = prof[k, v:v + 2, :]
            if k == 0:
                inv = 1.0 / (1.0 + below)
                off = x * inv
            else:
                inv = 1.0 / (1.0 + above * (1.0 - factor) + below)
                off = (x + above * off) * inv
            factor = below * inv
            above = below
            off_all[k, v:v + 2, :] = off
            fac[k, v:v + 2, :] = factor
        return off, factor, below

    off, factor, below = eliminate(0, 0, True)
    code = (local + 1).astype(F32)
    blank = jnp.zeros_like(code)
    even = jnp.concatenate([off[0:1], factor[0:1], code, blank], axis=0)
    odd = jnp.concatenate([off[1:2], below[1:2], code, blank], axis=0)
    wide = jnp.concatenate([
        jnp.concatenate(halves(even), axis=0), jnp.concatenate(halves(odd), axis=0)], axis=1)
    owner8 = jnp.broadcast_to(owner, (8, cols))

    def dispatch(g, c):
        for t in range(GROUP // 2):
            parts = []
            for u in range(2):
                m = owner8 == g * GROUP + 2 * t + u
                parts.append(jnp.where(jnp.concatenate([m, m], axis=1), wide, 0.0))
            lhs[pl.ds(16 * t, 16), :] = jnp.concatenate(parts, axis=0).astype(BF16)
        out = dot(lhs[...], rout[0:LANES, :], NT)
        for d in range(GROUP):
            send1[g * GROUP + d] = out[8 * d:8 * d + 4] + out[8 * d + 4:8 * d + 8]
        return c

    each(groups, dispatch, 0)

    pl.semaphore_wait(barrier, n - 1)

    def send(src, dst, ss, rs):
        def one(o):
            q = peer(o)
            pltpu.make_async_remote_copy(
                src_ref=src.at[q], dst_ref=dst.at[me], send_sem=ss, recv_sem=rs,
                device_id=q, device_id_type=pl.DeviceIdType.LOGICAL).start()
        peers(one)

    def wait_all(buf, sem):
        part = buf.at[pl.ds(0, n - 1)]
        pltpu.make_async_copy(part, part, sem).wait()

    send(send1, recv1, s1, r1.at[mine])
    pltpu.make_async_copy(send1.at[me], recv1.at[me], r1.at[mine]).start()

    eliminate(1, 2, False)
    for c in loads[1:]:
        c.wait()
    present = jnp.concatenate(
        [jnp.ones((1, cols), F32), flag[...].astype(F32)], axis=0)
    share = frac[...] * present
    share = share / jnp.sum(share, axis=0, keepdims=True)

    lane = lax.broadcasted_iota(I32, (4, LANES), 1)
    left = lane < HALF
    slots = crew * HALF

    def collect(i, acc):
        first = crew_at(i) * crew
        part = recv1.at[pl.ds(first, crew)]
        pltpu.make_async_copy(part, part, r1.at[crew_at(i)]).wait()
        evens, odds = [], []
        for m in range(crew // 2):
            a = recv1[first + 2 * m]
            b = recv1[first + 2 * m + 1]
            evens.append(jnp.where(left, a, pltpu.roll(b, HALF, 1)))
            odds.append(jnp.where(left, pltpu.roll(a, HALF, 1), b))
        even = jnp.concatenate(evens, axis=1)
        odd = jnp.concatenate(odds, axis=1)
        at = even[2:3].astype(I32) - 1
        high, low = halves(jnp.concatenate([even[0:2], odd[0:2]], axis=0))
        v = jnp.concatenate([high, low], axis=0)
        at8 = jnp.broadcast_to(at, (8, slots))
        far = at8 // LANES
        far = jnp.where(at8 < 0, -1, far)
        code_h[i] = far
        within = at - far[0:1] * LANES
        jl = one_hot(lax.broadcasted_iota(I32, (LANES, slots), 0) == within)
        near[i] = jl
        rows = jnp.concatenate(
            [jnp.where(far == h, v, 0.0) for h in range(blocks)], axis=0).astype(BF16)
        return acc + dot(rows, jl, NT)

    got = each(gx, collect, jnp.zeros((8 * blocks, LANES), F32))
    x = jnp.concatenate(
        [got[8 * h:8 * h + 4] + got[8 * h + 4:8 * h + 8] for h in range(blocks)], axis=1)
    kinds = base.shape[0]
    off_h, fac_s, off_m, exch = [jnp.broadcast_to(x[i:i + 1], (kinds, cols)) for i in range(4)]
    bottom = base[...]
    absorbed = flux[...]
    coupled = link[...]
    temp = bottom
    for _ in range(SWEEPS):
        sat = 0.6 * jnp.exp(0.3 * temp)
        mean_heat = jnp.sum(share * temp, axis=0, keepdims=True)
        mean_moist = jnp.sum(share * sat, axis=0, keepdims=True)
        air_heat = off_h + fac_s * mean_heat
        air_moist = off_m + fac_s * mean_moist
        emitted = 0.5 * jnp.exp(0.2 * temp)
        imbalance = (absorbed - emitted - exch * (temp - air_heat)
                     - 2.5 * exch * (sat - air_moist) - coupled * (temp - bottom))
        slope = 0.2 * emitted + exch * (1.0 + 2.5 * 0.3 * sat) + coupled
        temp = temp + imbalance / slope
    kelvin[...] = temp
    sat = 0.6 * jnp.exp(0.3 * temp)
    mean_heat = jnp.sum(share * temp, axis=0, keepdims=True)
    mean_moist = jnp.sum(share * sat, axis=0, keepdims=True)
    reply = jnp.concatenate([mean_heat, mean_moist, drift[...]], axis=0)
    reply = jnp.concatenate(halves(reply), axis=0)
    reply = jnp.concatenate(
        [reply[:, h * LANES:(h + 1) * LANES] for h in range(blocks)], axis=0).astype(BF16)
    left2 = lax.broadcasted_iota(I32, (2, LANES), 1) < HALF

    def answer(i, c):
        first = crew_at(i) * crew
        raw = dot(reply, near[i], NN)
        far = code_h[i]
        y = jnp.zeros((8, slots), F32)
        for h in range(blocks):
            y = y + jnp.where(far == h, raw[8 * h:8 * h + 8], 0.0)
        y = y[0:4] + y[4:8]
        for m in range(crew // 2):
            tile = y[:, m * LANES:(m + 1) * LANES]
            turned = pltpu.roll(tile, HALF, 1)
            send2[first + 2 * m] = jnp.where(left2, tile[0:2], turned[2:4])
            send2[first + 2 * m + 1] = jnp.where(left2, turned[0:2], tile[2:4])
        return c

    each(gx, answer, 0)
    recv2[me] = send2[me]
    send(send2, recv2, s2, r2)
    wait_all(recv2, r2)

    row = lax.broadcasted_iota(I32, (8, cols), 0) // 2
    shifted = owner8 - row

    def gather(g, acc):
        r = jnp.concatenate([recv2[g * GROUP + d] for d in range(GROUP)], axis=0)
        high, low = halves(r)
        both = jnp.concatenate([high, low], axis=1).astype(BF16)
        raw = dot(both, rout[...], NN)
        for t in range(GROUP // 4):
            m = shifted == g * GROUP + 4 * t
            acc = acc + jnp.where(jnp.concatenate([m, m], axis=1), raw[8 * t:8 * t + 8], 0.0)
        return acc

    acc = each(groups, gather, jnp.zeros((8, 2 * cols), F32))
    acc = acc[0:4] + acc[4:8]
    acc = acc[0:2] + acc[2:4]
    boundary[...] = jnp.concatenate([acc[:, :cols], acc[:, cols:]], axis=0)
    wait_all(send1, s1)
    wait_all(send2, s2)


def finish(pieces, off, fac, boundary, kelvin, adv_hbm, kelvin_hbm, adv, out_sem, kelvin_sem):
    levels = off.shape[0]
    step = levels // pieces
    kelvin_out = pltpu.make_async_copy(kelvin, kelvin_hbm, kelvin_sem)
    kelvin_out.start()
    value = boundary[...]
    outs = []
    for k in reversed(range(levels)):
        value = off[k] + fac[k] * value
        adv[k] = value
        if k % step == 0:
            rows = pl.ds(k, step)
            outs.append(pltpu.make_async_copy(
                adv.at[rows], adv_hbm.at[rows], out_sem.at[k // step]))
            outs[-1].start()
    kelvin_out.wait()
    for c in outs:
        c.wait()


def per_device(sizes, *args):
    gx, gy, sa = sizes
    n = gx * gy * sa
    levels, fields, cols = args[0].shape
    kinds = args[7].shape[0]
    assert n % GROUP == 0 and 2 * cols // n <= HALF and cols % LANES == 0
    groups = n // GROUP
    pieces = 4 if levels % 4 == 0 else 1
    vmem = [pltpu.VMEM(a.shape, a.dtype) for a in args]
    off, fac, boundary, kelvin = pl.pallas_call(
        functools.partial(kernel, (gx, gy, sa, levels, cols, pieces)),
        out_shape=(
            pltpu.VMEM(args[0].shape, F32),
            pltpu.VMEM(args[0].shape, F32),
            pltpu.VMEM((fields, cols), F32),
            pltpu.VMEM((kinds, cols), F32),
        ),
        in_specs=[pl.BlockSpec(memory_space=pltpu.HBM)] * len(args),
        out_specs=[pl.BlockSpec(memory_space=pltpu.VMEM)] * 4,
        scratch_shapes=vmem + [
            pltpu.VMEM((2 * LANES, 2 * cols), BF16),
            pltpu.VMEM((8 * GROUP, 2 * cols), BF16),
            pltpu.VMEM((gx, LANES, n // gx * HALF), BF16),
            pltpu.VMEM((gx, 8, n // gx * HALF), I32),
            pltpu.VMEM((n, 4, LANES), F32),
            pltpu.VMEM((n, 4, LANES), F32),
            pltpu.VMEM((n, 2, LANES), F32),
            pltpu.VMEM((n, 2, LANES), F32),
            pltpu.SemaphoreType.DMA((7,)),
            pltpu.SemaphoreType.DMA((2, pieces)),
            pltpu.SemaphoreType.DMA,
            pltpu.SemaphoreType.DMA((gx,)),
            pltpu.SemaphoreType.DMA,
            pltpu.SemaphoreType.DMA,
        ],
        compiler_params=pltpu.CompilerParams(
            collective_id=0, has_side_effects=True, vmem_limit_bytes=VMEM_GRANT),
    )(*args)
    return pl.pallas_call(
        functools.partial(finish, pieces),
        out_shape=(
            jax.ShapeDtypeStruct(args[0].shape, F32),
            jax.ShapeDtypeStruct((kinds, cols), F32),
        ),
        in_specs=[pl.BlockSpec(memory_space=pltpu.VMEM)] * 4,
        out_specs=[pl.BlockSpec(memory_space=pltpu.HBM)] * 2,
        scratch_shapes=[
            pltpu.VMEM(args[0].shape, F32),
            pltpu.SemaphoreType.DMA((pieces,)),
            pltpu.SemaphoreType.DMA,
        ],
        compiler_params=pltpu.CompilerParams(vmem_limit_bytes=FINISH_GRANT),
    )(off, fac, boundary, kelvin)


def solution(mesh):
    wide = P(None, None, AXES)
    flat = P(None, AXES)
    return jax.shard_map(
        functools.partial(per_device, tuple(mesh.shape[a] for a in AXES)),
        mesh=mesh,
        in_specs=(wide, wide) + (flat,) * 7,
        out_specs=(wide, flat),
        check_vma=False,
    )
```

```python
import functools

import jax
import jax.numpy as jnp
from jax import lax
from jax.experimental import pallas as pl
from jax.experimental.pallas import tpu as pltpu
from jax.sharding import PartitionSpec as P

SWEEPS = 3
AXES = ("gx", "gy", "sa")
LANES = 128
HALF = LANES // 2
GROUP = 32
F32, BF16, I32 = jnp.float32, jnp.bfloat16, jnp.int32
VMEM_GRANT = 60 * 1024 * 1024
FINISH_GRANT = 4 * 1024 * 1024
NT = (((1,), (1,)), ((), ()))
NN = (((1,), (0,)), ((), ()))


def dot(a, b, dims):
    return lax.dot_general(a, b, dims, preferred_element_type=F32)


def halves(x):
    high = x.astype(BF16).astype(F32)
    return high, x - high


def one_hot(mask):
    return jnp.where(mask, 1.0, 0.0).astype(BF16)


def kernel(
    sizes,
    prof_hbm, turb_hbm, owner_hbm, frac_hbm, flag_hbm, flux_hbm, link_hbm, base_hbm, drift_hbm,
    off_all, fac, boundary, kelvin,
    prof, turb, owner_v, frac, flag, flux, link, base, drift,
    rout, lhs, near, code_h, send1, recv1, send2, recv2,
    in_sem, lev_sem, s1, r1, s2, r2,
):
    gx, gy, sa, levels, cols, pieces = sizes
    n = gx * gy * sa
    blocks = cols // LANES
    groups = n // GROUP
    step = levels // pieces
    me = (lax.axis_index("gx") * gy + lax.axis_index("gy")) * sa + lax.axis_index("sa")

    mine = lax.axis_index("gx")
    upper = 2 * mine >= gx
    crew = n // gx

    def peer(t):
        q = jnp.where(upper, t, n - 2 - t)
        return q + jnp.where(q >= me, 1, 0)

    def peers(fn, start=0, count=n - 1):
        if n <= GROUP:
            for o in range(count):
                fn(start + o)
        else:
            def body(o, c):
                fn(o)
                return c
            lax.fori_loop(start, start + count, body, 0)

    def each(count, fn, init):
        if count > 4:
            return lax.fori_loop(0, count, fn, init)
        for i in range(count):
            init = fn(i, init)
        return init

    def crew_at(i):
        return jnp.where(upper, gx - 1 - i, i)

    loads = [
        pltpu.make_async_copy(a, b, in_sem.at[i])
        for i, (a, b) in enumerate((
            (owner_hbm, owner_v), (frac_hbm, frac), (flag_hbm, flag), (flux_hbm, flux),
            (link_hbm, link), (base_hbm, base), (drift_hbm, drift)))
    ]
    loads[0].start()
    lev_loads = []
    for i in range(pieces):
        rows = pl.ds(i * step, step)
        lev_loads.append((
            pltpu.make_async_copy(turb_hbm.at[rows], turb.at[rows], lev_sem.at[0, i]),
            pltpu.make_async_copy(prof_hbm.at[rows], prof.at[rows], lev_sem.at[1, i])))
        for c in lev_loads[-1]:
            c.start()
    for c in loads[1:]:
        c.start()

    barrier = pltpu.get_barrier_semaphore()
    peers(lambda o: pl.semaphore_signal(
        barrier, inc=1, device_id=peer(o), device_id_type=pl.DeviceIdType.LOGICAL))

    loads[0].wait()
    owner = owner_v[0:1, :]
    local = owner_v[1:2, :]
    onehot_d = lax.broadcasted_iota(I32, (n, cols), 0) == owner
    d01 = one_hot(onehot_d)
    stacked = jnp.concatenate([d01[:, b * LANES:(b + 1) * LANES] for b in range(blocks)], axis=0)
    ti = lax.broadcasted_iota(I32, (LANES, 2 * LANES), 0)
    tj = lax.broadcasted_iota(I32, (LANES, 2 * LANES), 1)
    tri = one_hot((ti < tj) | (tj >= LANES))
    counts = dot(stacked, tri, NN)
    carry = jnp.zeros((n, LANES), F32)
    ranks = []
    for b in range(blocks):
        part = counts[b * n:(b + 1) * n]
        mask = onehot_d[:, b * LANES:(b + 1) * LANES]
        ranks.append(jnp.sum(jnp.where(mask, part[:, :LANES] + carry, 0.0), axis=0, keepdims=True))
        carry = carry + part[:, LANES:]
    rank = jnp.concatenate(ranks, axis=1).astype(I32)
    r01 = one_hot(lax.broadcasted_iota(I32, (HALF, cols), 0) == rank)
    zero = jnp.zeros((HALF, cols), BF16)
    for i in range(2):
        rout[pl.ds(i * LANES, HALF), 0:cols] = r01
        rout[pl.ds(i * LANES, HALF), cols:2 * cols] = zero
        rout[pl.ds(i * LANES + HALF, HALF), 0:cols] = zero
        rout[pl.ds(i * LANES + HALF, HALF), cols:2 * cols] = r01

    def eliminate(row, v, wait):
        above = off = factor = None
        for k in range(levels):
            if wait and k % step == 0:
                for c in lev_loads[k // step]:
                    c.wait()
            below = jnp.broadcast_to(turb[k, row:row + 1, :], (2, cols))
            x = prof[k, v:v + 2, :]
            if k == 0:
                inv = 1.0 / (1.0 + below)
                off = x * inv
            else:
                inv = 1.0 / (1.0 + above * (1.0 - factor) + below)
                off = (x + above * off) * inv
            factor = below * inv
            above = below
            off_all[k, v:v + 2, :] = off
            fac[k, v:v + 2, :] = factor
        return off, factor, below

    off, factor, below = eliminate(0, 0, True)
    code = (local + 1).astype(F32)
    blank = jnp.zeros_like(code)
    even = jnp.concatenate([off[0:1], factor[0:1], code, blank], axis=0)
    odd = jnp.concatenate([off[1:2], below[1:2], code, blank], axis=0)
    wide = jnp.concatenate([
        jnp.concatenate(halves(even), axis=0), jnp.concatenate(halves(odd), axis=0)], axis=1)
    owner8 = jnp.broadcast_to(owner, (8, cols))

    def dispatch(g, c):
        for t in range(GROUP // 2):
            parts = []
            for u in range(2):
                m = owner8 == g * GROUP + 2 * t + u
                parts.append(jnp.where(jnp.concatenate([m, m], axis=1), wide, 0.0))
            lhs[pl.ds(16 * t, 16), :] = jnp.concatenate(parts, axis=0).astype(BF16)
        out = dot(lhs[...], rout[0:LANES, :], NT)
        for d in range(GROUP):
            send1[g * GROUP + d] = out[8 * d:8 * d + 4] + out[8 * d + 4:8 * d + 8]
        return c

    each(groups, dispatch, 0)

    pl.semaphore_wait(barrier, n - 1)

    def send(src, dst, ss, rs, start=0, count=n - 1):
        def one(o):
            q = peer(o)
            pltpu.make_async_remote_copy(
                src_ref=src.at[q], dst_ref=dst.at[me], send_sem=ss, recv_sem=rs,
                device_id=q, device_id_type=pl.DeviceIdType.LOGICAL).start()
        peers(one, start, count)

    def wait_all(buf, sem):
        part = buf.at[pl.ds(0, n - 1)]
        pltpu.make_async_copy(part, part, sem).wait()

    send(send1, recv1, s1, r1.at[mine])
    pltpu.make_async_copy(send1.at[me], recv1.at[me], r1.at[mine]).start()

    eliminate(1, 2, False)
    for c in loads[1:]:
        c.wait()
    present = jnp.concatenate(
        [jnp.ones((1, cols), F32), flag[...].astype(F32)], axis=0)
    share = frac[...] * present
    share = share / jnp.sum(share, axis=0, keepdims=True)

    lane = lax.broadcasted_iota(I32, (4, LANES), 1)
    left = lane < HALF
    slots = crew * HALF

    def collect(i, acc):
        first = crew_at(i) * crew
        part = recv1.at[pl.ds(first, crew)]
        pltpu.make_async_copy(part, part, r1.at[crew_at(i)]).wait()
        evens, odds = [], []
        for m in range(crew // 2):
            a = recv1[first + 2 * m]
            b = recv1[first + 2 * m + 1]
            evens.append(jnp.where(left, a, pltpu.roll(b, HALF, 1)))
            odds.append(jnp.where(left, pltpu.roll(a, HALF, 1), b))
        even = jnp.concatenate(evens, axis=1)
        odd = jnp.concatenate(odds, axis=1)
        at = even[2:3].astype(I32) - 1
        high, low = halves(jnp.concatenate([even[0:2], odd[0:2]], axis=0))
        v = jnp.concatenate([high, low], axis=0)
        at8 = jnp.broadcast_to(at, (8, slots))
        far = at8 // LANES
        far = jnp.where(at8 < 0, -1, far)
        code_h[i] = far
        within = at - far[0:1] * LANES
        jl = one_hot(lax.broadcasted_iota(I32, (LANES, slots), 0) == within)
        near[i] = jl
        rows = jnp.concatenate(
            [jnp.where(far == h, v, 0.0) for h in range(blocks)], axis=0).astype(BF16)
        return acc + dot(rows, jl, NT)

    got = each(gx, collect, jnp.zeros((8 * blocks, LANES), F32))
    x = jnp.concatenate(
        [got[8 * h:8 * h + 4] + got[8 * h + 4:8 * h + 8] for h in range(blocks)], axis=1)
    kinds = base.shape[0]
    off_h, fac_s, off_m, exch = [jnp.broadcast_to(x[i:i + 1], (kinds, cols)) for i in range(4)]
    bottom = base[...]
    absorbed = flux[...]
    coupled = link[...]
    temp = bottom
    for _ in range(SWEEPS):
        sat = 0.6 * jnp.exp(0.3 * temp)
        mean_heat = jnp.sum(share * temp, axis=0, keepdims=True)
        mean_moist = jnp.sum(share * sat, axis=0, keepdims=True)
        air_heat = off_h + fac_s * mean_heat
        air_moist = off_m + fac_s * mean_moist
        emitted = 0.5 * jnp.exp(0.2 * temp)
        imbalance = (absorbed - emitted - exch * (temp - air_heat)
                     - 2.5 * exch * (sat - air_moist) - coupled * (temp - bottom))
        slope = 0.2 * emitted + exch * (1.0 + 2.5 * 0.3 * sat) + coupled
        temp = temp + imbalance / slope
    kelvin[...] = temp
    sat = 0.6 * jnp.exp(0.3 * temp)
    mean_heat = jnp.sum(share * temp, axis=0, keepdims=True)
    mean_moist = jnp.sum(share * sat, axis=0, keepdims=True)
    reply = jnp.concatenate([mean_heat, mean_moist, drift[...]], axis=0)
    reply = jnp.concatenate(halves(reply), axis=0)
    reply = jnp.concatenate(
        [reply[:, h * LANES:(h + 1) * LANES] for h in range(blocks)], axis=0).astype(BF16)
    left2 = lax.broadcasted_iota(I32, (2, LANES), 1) < HALF

    def answer(i, c):
        first = crew_at(i) * crew
        raw = dot(reply, near[i], NN)
        far = code_h[i]
        y = jnp.zeros((8, slots), F32)
        for h in range(blocks):
            y = y + jnp.where(far == h, raw[8 * h:8 * h + 8], 0.0)
        y = y[0:4] + y[4:8]
        for m in range(crew // 2):
            tile = y[:, m * LANES:(m + 1) * LANES]
            turned = pltpu.roll(tile, HALF, 1)
            send2[first + 2 * m] = jnp.where(left2, tile[0:2], turned[2:4])
            send2[first + 2 * m + 1] = jnp.where(left2, turned[0:2], tile[2:4])
        return c

    def answer_far(c, carry):
        answer(gx - 1 - c, 0)
        send(send2, recv2, s2, r2, c * crew, crew)
        return carry

    far_planes = gx // 2
    each(far_planes, answer_far, 0)
    each(gx - far_planes, answer, 0)
    recv2[me] = send2[me]
    send(send2, recv2, s2, r2, far_planes * crew, n - 1 - far_planes * crew)
    wait_all(recv2, r2)

    row = lax.broadcasted_iota(I32, (8, cols), 0) // 2
    shifted = owner8 - row

    def gather(g, acc):
        r = jnp.concatenate([recv2[g * GROUP + d] for d in range(GROUP)], axis=0)
        high, low = halves(r)
        both = jnp.concatenate([high, low], axis=1).astype(BF16)
        raw = dot(both, rout[...], NN)
        for t in range(GROUP // 4):
            m = shifted == g * GROUP + 4 * t
            acc = acc + jnp.where(jnp.concatenate([m, m], axis=1), raw[8 * t:8 * t + 8], 0.0)
        return acc

    acc = each(groups, gather, jnp.zeros((8, 2 * cols), F32))
    acc = acc[0:4] + acc[4:8]
    acc = acc[0:2] + acc[2:4]
    boundary[...] = jnp.concatenate([acc[:, :cols], acc[:, cols:]], axis=0)
    wait_all(send1, s1)
    wait_all(send2, s2)


def finish(pieces, off, fac, boundary, kelvin, adv_hbm, kelvin_hbm, adv, out_sem, kelvin_sem):
    levels = off.shape[0]
    step = levels // pieces
    kelvin_out = pltpu.make_async_copy(kelvin, kelvin_hbm, kelvin_sem)
    kelvin_out.start()
    value = boundary[...]
    outs = []
    for k in reversed(range(levels)):
        value = off[k] + fac[k] * value
        adv[k] = value
        if k % step == 0:
            rows = pl.ds(k, step)
            outs.append(pltpu.make_async_copy(
                adv.at[rows], adv_hbm.at[rows], out_sem.at[k // step]))
            outs[-1].start()
    kelvin_out.wait()
    for c in outs:
        c.wait()


def per_device(sizes, *args):
    gx, gy, sa = sizes
    n = gx * gy * sa
    levels, fields, cols = args[0].shape
    kinds = args[7].shape[0]
    assert n % GROUP == 0 and 2 * cols // n <= HALF and cols % LANES == 0
    groups = n // GROUP
    pieces = 4 if levels % 4 == 0 else 1
    vmem = [pltpu.VMEM(a.shape, a.dtype) for a in args]
    off, fac, boundary, kelvin = pl.pallas_call(
        functools.partial(kernel, (gx, gy, sa, levels, cols, pieces)),
        out_shape=(
            pltpu.VMEM(args[0].shape, F32),
            pltpu.VMEM(args[0].shape, F32),
            pltpu.VMEM((fields, cols), F32),
            pltpu.VMEM((kinds, cols), F32),
        ),
        in_specs=[pl.BlockSpec(memory_space=pltpu.HBM)] * len(args),
        out_specs=[pl.BlockSpec(memory_space=pltpu.VMEM)] * 4,
        scratch_shapes=vmem + [
            pltpu.VMEM((2 * LANES, 2 * cols), BF16),
            pltpu.VMEM((8 * GROUP, 2 * cols), BF16),
            pltpu.VMEM((gx, LANES, n // gx * HALF), BF16),
            pltpu.VMEM((gx, 8, n // gx * HALF), I32),
            pltpu.VMEM((n, 4, LANES), F32),
            pltpu.VMEM((n, 4, LANES), F32),
            pltpu.VMEM((n, 2, LANES), F32),
            pltpu.VMEM((n, 2, LANES), F32),
            pltpu.SemaphoreType.DMA((7,)),
            pltpu.SemaphoreType.DMA((2, pieces)),
            pltpu.SemaphoreType.DMA,
            pltpu.SemaphoreType.DMA((gx,)),
            pltpu.SemaphoreType.DMA,
            pltpu.SemaphoreType.DMA,
        ],
        compiler_params=pltpu.CompilerParams(
            collective_id=0, has_side_effects=True, vmem_limit_bytes=VMEM_GRANT),
    )(*args)
    return pl.pallas_call(
        functools.partial(finish, pieces),
        out_shape=(
            jax.ShapeDtypeStruct(args[0].shape, F32),
            jax.ShapeDtypeStruct((kinds, cols), F32),
        ),
        in_specs=[pl.BlockSpec(memory_space=pltpu.VMEM)] * 4,
        out_specs=[pl.BlockSpec(memory_space=pltpu.HBM)] * 2,
        scratch_shapes=[
            pltpu.VMEM(args[0].shape, F32),
            pltpu.SemaphoreType.DMA((pieces,)),
            pltpu.SemaphoreType.DMA,
        ],
        compiler_params=pltpu.CompilerParams(vmem_limit_bytes=FINISH_GRANT),
    )(off, fac, boundary, kelvin)


def solution(mesh):
    wide = P(None, None, AXES)
    flat = P(None, AXES)
    return jax.shard_map(
        functools.partial(per_device, tuple(mesh.shape[a] for a in AXES)),
        mesh=mesh,
        in_specs=(wide, wide) + (flat,) * 7,
        out_specs=(wide, flat),
        check_vma=False,
    )
```
